512 devices in a mesh: dp: 64 (over x, z, core), refl: 8 (over y).
Axes of the slice: x: 4, y: 8, z: 8, core: 2. Of those that a mesh axis runs over, the one named last changes fastest.
Arguments:
- intensities: bfloat16 [2048, 16384], P('dp', 'refl'), may hold values from -12 to 12
- observed: int32 [2048, 16384], P('dp', 'refl'), may hold values 0 or 1
- qweights: bfloat16 [2048, 16384], P('dp', 'refl'), may hold values from 0.25 to 4
- ops: int32 [4, 16384], P(None, 'refl'), may hold values from 0 to 16383, as said below
- pick: int32 [64, 64], P(None, 'dp'), may hold values from 0 to 7
Outputs:
- corr: float32 [4, 2048, 256], P(None, ('dp', 'refl'))
- returned: float32 [4, 64, 64, 4, 32], P(None, 'dp', None, None, 'refl')
The draws below stay inside these ranges and needn't reach their ends.
Inputs may be any that keep to these rules, and one draw needn't show every extreme that they name: Each row of ops is a permutation of the reflections that maps every aligned block of 2048 reflections onto itself.
All inputs are finite; a program needn't handle non-finite values. No bound on the sum of `observed` on one device may be relied on, other than what follows from the above.
Results may differ from the reference program's by a relative error of at most 0.0084.
Values may be sent and summed in bfloat16 or wider, within the bound.
A program may use at most 64 MiB of HBM per device.

```python
import math
import jax
import jax.numpy as jnp
from jax import lax

BLK = 32
SUB = 4
REFL = 16384
NOPS = 4
REFL_DEV = 2048
BLOCKS = 64
DATASETS = 2048


def draw_intensities(key, part):
    first, second, third = jax.random.split(jax.random.fold_in(key, 11), 3)
    common = jax.random.normal(first, (1, REFL), jnp.float32)
    amplitude = jax.random.uniform(second, (DATASETS, 1), jnp.float32, -1.5, 1.5)
    noise = 0.8 * jax.random.normal(third, (DATASETS, REFL), jnp.float32)
    values = amplitude * common + noise
    return jnp.clip(values, -12.0, 12.0).astype(jnp.bfloat16)


def draw_ops(key, part):
    parts_count = REFL // REFL_DEV
    keys = jax.random.split(jax.random.fold_in(key, 23), NOPS * parts_count)
    perms = jax.vmap(lambda single: jax.random.permutation(single, REFL_DEV))(keys)
    perms = perms.reshape(NOPS, parts_count, REFL_DEV).astype(jnp.int32)
    offsets = (jnp.arange(parts_count, dtype=jnp.int32) * REFL_DEV)[None, :, None]
    return (perms + offsets).reshape(NOPS, REFL)


def place_ends(result, own_key, least, high):
    longest = result.shape.index(max(result.shape))
    spots = []
    for shift in (0, 1):
        where = [jax.random.randint(jax.random.fold_in(own_key, axis), (), 0, length) for axis, length in enumerate(result.shape)]
        where[longest] = (where[longest] + shift) % result.shape[longest]
        spots.append(tuple(where))
    return result.at[spots[0]].set(least).at[spots[1]].set(high)


def levels(own_key, extent, shards, low, largest):
    level, own = 1.0, jax.random.fold_in(own_key, 6)
    for position, shards_of in shards:
        steps = jnp.exp(jax.random.uniform(jax.random.fold_in(own, position), (shards_of,), jnp.float32, low / len(shards), largest / len(shards)))
        level = level * jnp.repeat(steps, extent[position] // shards_of).reshape([-1 if axis == position else 1 for axis in range(len(extent))])
    return level


def setup_inputs(seed: int = 0) -> dict:
    arg_keys = jax.random.split(jax.random.key(seed), 6)
    return {
        "intensities": draw_intensities(jax.random.fold_in(arg_keys[5], 71), 0),
        "observed": place_ends((jax.random.randint(arg_keys[1], (DATASETS, REFL), 0, 2) < 1).astype(jnp.int32), jax.random.fold_in(arg_keys[1], 1), 0, 1),
        "qweights": jnp.clip(jnp.exp(math.log(4.0) - 2.7725887 * jax.random.uniform(arg_keys[2], (DATASETS, REFL), jnp.float32) ** levels(arg_keys[2], (DATASETS, REFL), ((0, 64), (1, 8)), -0.2, 0.2)), 0.25, 4.0).astype(jnp.bfloat16),
        "ops": draw_ops(jax.random.fold_in(arg_keys[5], 71), 0),
        "pick": place_ends(jax.random.randint(arg_keys[4], (BLOCKS, BLOCKS), 0, BLK // SUB), jax.random.fold_in(arg_keys[4], 1), 0, (BLK // SUB) - 1).astype(jnp.int32),
    }


def gram(left, right):
    return jnp.dot(left.astype(jnp.float32), right.astype(jnp.float32).T, precision=lax.Precision.HIGHEST, preferred_element_type=jnp.float32)

def reference(intensities, observed, qweights, ops, pick):
    weights = observed.astype(jnp.float32) * qweights.astype(jnp.float32)
    values = intensities.astype(jnp.float32)
    own_w = weights.astype(jnp.bfloat16)
    own_wx = (weights * values).astype(jnp.bfloat16)
    own_wxx = (weights * values * values).astype(jnp.bfloat16)
    blocks = DATASETS // BLK
    source = (jnp.arange(blocks, dtype=jnp.int32) * BLK)[None, :, None] + pick[:, :, None] * SUB + jnp.arange(SUB, dtype=jnp.int32)[None, None, :]
    source = source.reshape(blocks, blocks * SUB)

    def per_block(index):
        rows = source[index]
        part_w = own_w[rows]
        part_x = intensities[rows]
        start = (index * BLK).astype(jnp.int32)
        left_w = lax.dynamic_slice_in_dim(own_w, start, BLK, 0)
        left_wx = lax.dynamic_slice_in_dim(own_wx, start, BLK, 0)
        left_wxx = lax.dynamic_slice_in_dim(own_wxx, start, BLK, 0)
        results = []
        for k in range(NOPS):
            perm = ops[k]
            moved_w = part_w[:, perm]
            wide_w = moved_w.astype(jnp.float32)
            wide_x = part_x[:, perm].astype(jnp.float32)
            moved_wy = (wide_w * wide_x).astype(jnp.bfloat16)
            moved_wyy = (wide_w * wide_x * wide_x).astype(jnp.bfloat16)
            total_w = gram(left_w, moved_w)
            sum_x = gram(left_wx, moved_w)
            sum_xx = gram(left_wxx, moved_w)
            sum_y = gram(left_w, moved_wy)
            sum_xy = gram(left_wx, moved_wy)
            sum_yy = gram(left_w, moved_wyy)
            numer = total_w * sum_xy - sum_x * sum_y
            var_x = jnp.maximum(total_w * sum_xx - sum_x * sum_x, 0.05 * total_w * sum_xx)
            var_y = jnp.maximum(total_w * sum_yy - sum_y * sum_y, 0.05 * total_w * sum_yy)
            results.append(numer / jnp.sqrt(var_x * var_y))
        return jnp.stack(results, 0)
    out = lax.map(per_block, jnp.arange(blocks, dtype=jnp.int32))
    corr = jnp.transpose(out, (1, 0, 2, 3)).reshape(NOPS, DATASETS, blocks * SUB)
    returned = jnp.transpose(corr.reshape(NOPS, blocks, BLK, blocks, SUB), (0, 3, 1, 4, 2))
    return (corr, returned)
```

```python
import jax
import jax.numpy as jnp
from jax import lax
from jax.sharding import PartitionSpec as P

SUB = 4
NOPS = 4


def gram(left, right):
    return lax.dot_general(
        left, right, (((1,), (1,)), ((), ())), preferred_element_type=jnp.float32
    )


def pearson(total_w, sum_x, sum_xx, sum_y, sum_xy, sum_yy):
    numer = total_w * sum_xy - sum_x * sum_y
    var_x = jnp.maximum(total_w * sum_xx - sum_x * sum_x, 0.05 * total_w * sum_xx)
    var_y = jnp.maximum(total_w * sum_yy - sum_y * sum_y, 0.05 * total_w * sum_yy)
    return numer / jnp.sqrt(var_x * var_y)


def shards(intensities, observed, qweights, ops, pick):
    blk, width = intensities.shape
    groups = lax.axis_size("dp")
    shares = lax.axis_size("refl")
    rows = blk // shares
    own_w = (observed.astype(jnp.float32) * qweights.astype(jnp.float32)).astype(jnp.bfloat16)
    both = jnp.concatenate([intensities, own_w], 0)
    request = pick[:, 0][:, None] * SUB + jnp.arange(SUB, dtype=jnp.int32)[None, :]
    request = jnp.concatenate([request, request + blk], 1).reshape(-1)
    chosen = (request[:, None] == jnp.arange(2 * blk, dtype=jnp.int32)[None, :]).astype(jnp.bfloat16)
    send = jnp.dot(chosen, both, preferred_element_type=jnp.float32).astype(jnp.bfloat16)
    send = send.reshape(groups, 2 * SUB, width)
    got = lax.all_to_all(send, "dp", split_axis=0, concat_axis=0, tiled=True)
    local_ops = ops - lax.axis_index("refl") * width
    place = (local_ops[:, None, :] == jnp.arange(width, dtype=jnp.int32)[None, :, None]).astype(jnp.bfloat16)
    moved = jnp.einsum("ih,kgh->kig", both, place, preferred_element_type=jnp.float32)
    moved_x = moved[:, :blk]
    moved_w = moved[:, blk:]
    left_w = moved_w.astype(jnp.bfloat16).reshape(NOPS * blk, width)
    left_wx = (moved_w * moved_x).astype(jnp.bfloat16).reshape(NOPS * blk, width)
    left_wxx = (moved_w * moved_x * moved_x).astype(jnp.bfloat16).reshape(NOPS * blk, width)
    left = jnp.concatenate([left_w, left_wx, left_wxx], 0)
    got_x = got[:, :SUB].reshape(groups * SUB, width).astype(jnp.float32)
    got_w = got[:, SUB:].reshape(groups * SUB, width)
    wide_w = got_w.astype(jnp.float32)
    right_wy = (wide_w * got_x).astype(jnp.bfloat16)
    right_wyy = (wide_w * got_x * got_x).astype(jnp.bfloat16)
    n = NOPS * blk
    first = gram(left, got_w)
    second = gram(left[: 2 * n], right_wy)
    third = gram(left[:n], right_wyy)
    stats = jnp.concatenate([first, second, third], 0)
    stats = stats.reshape(6 * NOPS, shares, rows, groups * SUB)
    share = lax.psum_scatter(stats, "refl", scatter_dimension=1, tiled=False)
    share = share.reshape(6, NOPS, rows, groups * SUB)
    corr = pearson(*[share[i] for i in range(6)])
    outgoing = jnp.transpose(corr.reshape(NOPS, rows, groups, SUB), (0, 2, 3, 1))[:, :, None]
    returned = lax.all_to_all(outgoing, "dp", split_axis=1, concat_axis=2, tiled=True)
    return (corr, returned)


def solution(mesh):
    return jax.shard_map(
        shards,
        mesh=mesh,
        in_specs=(
            P("dp", "refl"),
            P("dp", "refl"),
            P("dp", "refl"),
            P(None, "refl"),
            P(None, "dp"),
        ),
        out_specs=(P(None, ("dp", "refl"), None), P(None, "dp", None, None, "refl")),
        check_vma=False,
    )
```

```python
import functools

import jax
import jax.numpy as jnp
from jax import lax
from jax.experimental import pallas as pl
from jax.experimental.pallas import tpu as pltpu
from jax.sharding import PartitionSpec as P

SUB = 4
NOPS = 4
MESH = pl.DeviceIdType.MESH


def gram(left, right):
    return lax.dot_general(
        left, right, (((1,), (1,)), ((), ())), preferred_element_type=jnp.float32
    )


def sums_kernel(left_ref, got_ref, out_ref):
    shares, _, cols = out_ref.shape
    groups = cols // SUB
    rows = got_ref.shape[0]
    got = got_ref[...]
    at = lax.broadcasted_iota(jnp.int32, (cols, rows), 0)
    source = lax.broadcasted_iota(jnp.int32, (cols, rows), 1)
    wanted = (at % groups) * (2 * SUB) + at // groups
    pick_x = (source == wanted).astype(jnp.float32).astype(jnp.bfloat16)
    pick_w = (source == wanted + SUB).astype(jnp.float32).astype(jnp.bfloat16)
    got_x = jnp.dot(pick_x, got, preferred_element_type=jnp.float32)
    got_w = jnp.dot(pick_w, got, preferred_element_type=jnp.float32)
    right_w = got_w.astype(jnp.bfloat16)
    wy = got_w * got_x
    right_wy = wy.astype(jnp.bfloat16)
    right_wyy = (wy * got_x).astype(jnp.bfloat16)
    left_w = left_ref[0]
    left_wx = left_ref[1]
    left_wxx = left_ref[2]
    parts = (
        gram(left_w, right_w),
        gram(left_wx, right_w),
        gram(left_wxx, right_w),
        gram(left_w, right_wy),
        gram(left_wx, right_wy),
        gram(left_w, right_wyy),
    )

    @pl.when(pl.program_id(0) == 0)
    def _():
        out_ref[...] = jnp.zeros_like(out_ref)

    for i, part in enumerate(parts):
        n = part.shape[0] // shares
        out_ref[:, i * n : (i + 1) * n, :] += part.reshape(shares, n, cols)


def six_sums(left, got, shares):
    width = left.shape[-1]
    rows = got.shape[0]
    tile = 512
    n = left.shape[1]
    return pl.pallas_call(
        sums_kernel,
        grid=(width // tile,),
        in_specs=[
            pl.BlockSpec((3, n, tile), lambda i: (0, 0, i)),
            pl.BlockSpec((rows, tile), lambda i: (0, i)),
        ],
        out_specs=pl.BlockSpec((shares, 6 * n // shares, rows // 2), lambda i: (0, 0, 0)),
        out_shape=jax.ShapeDtypeStruct((shares, 6 * n // shares, rows // 2), jnp.float32),
        compiler_params=pltpu.CompilerParams(vmem_limit_bytes=48 * 1024 * 1024),
    )(left, got)


def pearson(total_w, sum_x, sum_xx, sum_y, sum_xy, sum_yy):
    numer = total_w * sum_xy - sum_x * sum_y
    var_x = jnp.maximum(total_w * sum_xx - sum_x * sum_x, 0.05 * total_w * sum_xx)
    var_y = jnp.maximum(total_w * sum_yy - sum_y * sum_y, 0.05 * total_w * sum_yy)
    return numer / jnp.sqrt(var_x * var_y)


def finish_kernel(
    shares, groups, stats_ref, corr_ref, back_ref,
    held, msgs, landed, send_sem, recv_sem, out_sem, in_sem, own_sem,
):
    me_r = lax.axis_index("refl")
    me_d = lax.axis_index("dp")
    barrier = pltpu.get_barrier_semaphore()
    for t in range(1, shares):
        pl.semaphore_signal(
            barrier, inc=1, device_id={"refl": lax.rem(me_r + t, shares)}, device_id_type=MESH
        )

    @pl.loop(1, groups)
    def _(t):
        pl.semaphore_signal(
            barrier, inc=1, device_id={"dp": lax.rem(me_d + t, groups)}, device_id_type=MESH
        )

    pl.semaphore_wait(barrier, shares - 1 + groups - 1)
    copies = []
    for t in (4, 3, 5, 2, 6, 1, 7) if shares == 8 else range(1, shares):
        to = lax.rem(me_r + t, shares)
        copy = pltpu.make_async_remote_copy(
            src_ref=stats_ref.at[to],
            dst_ref=held.at[t - 1],
            send_sem=send_sem.at[t - 1],
            recv_sem=recv_sem.at[t - 1],
            device_id={"refl": to},
            device_id_type=MESH,
        )
        copy.start()
        copies.append((t, copy))
    total = stats_ref[me_r]
    for t, copy in sorted(copies, key=lambda c: min(c[0], shares - c[0])):
        copy.wait_recv()
        total = total + held[t - 1]
    n = total.shape[0] // 6
    corr = pearson(*[total[i * n : (i + 1) * n] for i in range(6)])
    corr_ref[...] = corr
    flipped = corr.T
    lined = jnp.concatenate(
        [flipped[u * groups : (u + 1) * groups] for u in range(SUB)]
        + [jnp.zeros((groups, 128 - SUB * n), jnp.float32)],
        1,
    )
    for s in range(groups):
        msgs[s] = lined[s : s + 1]
    own = pltpu.make_async_copy(msgs.at[me_d], landed.at[me_d], own_sem)
    own.start()

    @pl.loop(1, groups)
    def _(t):
        to = lax.rem(me_d + t, groups)
        pltpu.make_async_remote_copy(
            src_ref=msgs.at[to],
            dst_ref=landed.at[me_d],
            send_sem=out_sem,
            recv_sem=in_sem,
            device_id={"dp": to},
            device_id_type=MESH,
        ).start()

    for _, copy in copies:
        copy.wait_send()
    own.wait()
    some = pl.ds(0, groups - 1)
    pltpu.make_async_copy(msgs.at[some], msgs.at[some], out_sem).wait()
    pltpu.make_async_copy(landed.at[some], landed.at[some], in_sem).wait()
    back_ref[...] = landed[...]


def finish(stats, groups):
    shares, six, cols = stats.shape
    n = six // 6
    return pl.pallas_call(
        functools.partial(finish_kernel, shares, groups),
        out_shape=(
            jax.ShapeDtypeStruct((n, cols), jnp.float32),
            jax.ShapeDtypeStruct((groups, 1, 128), jnp.float32),
        ),
        in_specs=[pl.BlockSpec(memory_space=pltpu.VMEM)],
        out_specs=[pl.BlockSpec(memory_space=pltpu.VMEM)] * 2,
        scratch_shapes=[
            pltpu.VMEM((shares - 1, six, cols), jnp.float32),
            pltpu.VMEM((groups, 1, 128), jnp.float32),
            pltpu.VMEM((groups, 1, 128), jnp.float32),
            pltpu.SemaphoreType.DMA((shares - 1,)),
            pltpu.SemaphoreType.DMA((shares - 1,)),
            pltpu.SemaphoreType.DMA,
            pltpu.SemaphoreType.DMA,
            pltpu.SemaphoreType.DMA,
        ],
        compiler_params=pltpu.CompilerParams(collective_id=0, has_side_effects=True),
    )(stats)


def shards(intensities, observed, qweights, ops, pick):
    blk, width = intensities.shape
    groups = lax.axis_size("dp")
    shares = lax.axis_size("refl")
    rows = blk // shares
    own_w = (observed.astype(jnp.float32) * qweights.astype(jnp.float32)).astype(jnp.bfloat16)
    both = jnp.concatenate([intensities, own_w], 0)
    request = pick[:, 0][:, None] * SUB + jnp.arange(SUB, dtype=jnp.int32)[None, :]
    request = jnp.concatenate([request, request + blk], 1).reshape(-1)
    chosen = (request[:, None] == jnp.arange(2 * blk, dtype=jnp.int32)[None, :]).astype(jnp.bfloat16)
    send = jnp.dot(chosen, both, preferred_element_type=jnp.float32).astype(jnp.bfloat16)
    send = send.reshape(groups, 2 * SUB, width)
    got = lax.all_to_all(send, "dp", split_axis=0, concat_axis=0, tiled=True)
    local_ops = ops - lax.axis_index("refl") * width
    place = (local_ops[:, None, :] == jnp.arange(width, dtype=jnp.int32)[None, :, None]).astype(jnp.bfloat16)
    moved = jnp.einsum("ih,kgh->kig", both, place, preferred_element_type=jnp.float32)
    moved = moved.reshape(NOPS, 2, shares, rows, width).transpose(1, 2, 0, 3, 4)
    moved = moved.reshape(2, NOPS * blk, width)
    moved_x, moved_w = moved[0], moved[1]
    moved_wx = moved_w * moved_x
    left = jnp.stack([moved_w, moved_wx, moved_wx * moved_x], 0).astype(jnp.bfloat16)
    stats = six_sums(left, got.reshape(groups * 2 * SUB, width), shares)
    corr, back = finish(stats, groups)
    corr = corr.reshape(NOPS, rows, SUB, groups).transpose(0, 1, 3, 2)
    corr = corr.reshape(NOPS, rows, groups * SUB)
    back = back[:, 0, : SUB * NOPS * rows].reshape(groups, SUB, NOPS, rows)
    returned = back.transpose(2, 0, 1, 3)[:, None]
    return (corr, returned)


def solution(mesh):
    return jax.shard_map(
        shards,
        mesh=mesh,
        in_specs=(
            P("dp", "refl"),
            P("dp", "refl"),
            P("dp", "refl"),
            P(None, "refl"),
            P(None, "dp"),
        ),
        out_specs=(P(None, ("dp", "refl"), None), P(None, "dp", None, None, "refl")),
        check_vma=False,
    )
```

```python
import functools

import jax
import jax.numpy as jnp
from jax import lax
from jax.experimental import pallas as pl
from jax.experimental.pallas import tpu as pltpu
from jax.sharding import PartitionSpec as P

SUB = 4
NOPS = 4
MESH = pl.DeviceIdType.MESH


def gram(left, right):
    return lax.dot_general(
        left, right, (((1,), (1,)), ((), ())), preferred_element_type=jnp.float32
    )


def pearson(total_w, sum_x, sum_xx, sum_y, sum_xy, sum_yy):
    numer = total_w * sum_xy - sum_x * sum_y
    var_x = jnp.maximum(total_w * sum_xx - sum_x * sum_x, 0.05 * total_w * sum_xx)
    var_y = jnp.maximum(total_w * sum_yy - sum_y * sum_y, 0.05 * total_w * sum_yy)
    return numer / jnp.sqrt(var_x * var_y)


def whole_kernel(
    shares, groups, send_ref, both_ref, ops_ref, corr_ref, back_ref,
    landed, moved, left, stats, held, msgs, returned,
    send_sem, recv_sem, own_sem, part_send, part_recv, out_sem, in_sem, kept_sem,
):
    me_r = lax.axis_index("refl")
    me_d = lax.axis_index("dp")
    half = groups // 2
    me_s = me_d // 2
    me_c = lax.rem(me_d, 2)
    cores = (me_c, 1 - me_c)
    width = both_ref.shape[1]
    blk = both_ref.shape[0] // 2
    rows = blk // shares
    n = NOPS * rows
    barrier = pltpu.get_barrier_semaphore()
    for t in range(1, shares):
        pl.semaphore_signal(
            barrier, inc=1, device_id={"refl": lax.rem(me_r + t, shares)}, device_id_type=MESH
        )

    @pl.loop(1, groups)
    def _(t):
        pl.semaphore_signal(
            barrier, inc=1, device_id={"dp": lax.rem(me_d + t, groups)}, device_id_type=MESH
        )

    pl.semaphore_wait(barrier, shares - 1 + groups - 1)
    own = pltpu.make_async_copy(send_ref.at[me_d], landed.at[0, me_s], own_sem)
    own.start()
    for p in range(2):

        @pl.loop(1 - p, half)
        def _(t):
            to = lax.rem(me_s + t, half) * 2 + cores[p]
            pltpu.make_async_remote_copy(
                src_ref=send_ref.at[to],
                dst_ref=landed.at[p, me_s],
                send_sem=send_sem.at[p],
                recv_sem=recv_sem.at[p],
                device_id={"dp": to},
                device_id_type=MESH,
            ).start()

    both = both_ref[...]
    step = 256
    for k in range(NOPS):
        line = ops_ref[k : k + 1, :] - me_r * width

        @pl.loop(0, width // step)
        def _(g):
            at = lax.broadcasted_iota(jnp.int32, (step, width), 0) + g * step
            place = (at == line).astype(jnp.float32).astype(jnp.bfloat16)
            lanes = pl.ds(pl.multiple_of(g * step, step), step)
            put = gram(both, place).astype(jnp.bfloat16)
            moved[0, k * blk : (k + 1) * blk, lanes] = put[:blk]
            moved[1, k * blk : (k + 1) * blk, lanes] = put[blk:]

    to_row = lax.broadcasted_iota(jnp.int32, (NOPS * blk, NOPS * blk), 0)
    from_row = lax.broadcasted_iota(jnp.int32, (NOPS * blk, NOPS * blk), 1)
    want = ((to_row // rows) % NOPS) * blk + (to_row // n) * rows + to_row % rows
    order = (from_row == want).astype(jnp.float32).astype(jnp.bfloat16)
    tile = 512

    @pl.loop(0, width // tile)
    def _(g):
        lanes = pl.ds(pl.multiple_of(g * tile, tile), tile)
        own_x = jnp.dot(order, moved[0, :, lanes], preferred_element_type=jnp.float32)
        own_w = jnp.dot(order, moved[1, :, lanes], preferred_element_type=jnp.float32)
        own_wx = own_w * own_x
        left[0, :, lanes] = own_w.astype(jnp.bfloat16)
        left[1, :, lanes] = own_wx.astype(jnp.bfloat16)
        left[2, :, lanes] = (own_wx * own_x).astype(jnp.bfloat16)

    cols = half * SUB
    height = half * 2 * SUB
    at = lax.broadcasted_iota(jnp.int32, (cols, height), 0)
    source = lax.broadcasted_iota(jnp.int32, (cols, height), 1)
    wanted = (at % half) * (2 * SUB) + at // half
    pick_x = (source == wanted).astype(jnp.float32).astype(jnp.bfloat16)
    pick_w = (source == wanted + SUB).astype(jnp.float32).astype(jnp.bfloat16)
    copies = [[], []]
    for p in range(2):
        if p == 0:
            own.wait()
            some = pl.ds(0, half - 1)
            pltpu.make_async_copy(landed.at[0, some], landed.at[0, some], recv_sem.at[0]).wait()
        else:
            pltpu.make_async_copy(landed.at[1], landed.at[1], recv_sem.at[1]).wait()
        stats[p] = jnp.zeros(stats.shape[1:], jnp.float32)

        @pl.loop(0, width // tile)
        def _(g):
            lanes = pl.ds(pl.multiple_of(g * tile, tile), tile)
            got = landed[p, :, :, lanes].astype(jnp.float32).reshape(height, tile).astype(jnp.bfloat16)
            got_x = jnp.dot(pick_x, got, preferred_element_type=jnp.float32)
            got_w = jnp.dot(pick_w, got, preferred_element_type=jnp.float32)
            right_w = got_w.astype(jnp.bfloat16)
            wy = got_w * got_x
            right_wy = wy.astype(jnp.bfloat16)
            right_wyy = (wy * got_x).astype(jnp.bfloat16)
            left_w = left[0, :, lanes]
            left_wx = left[1, :, lanes]
            left_wxx = left[2, :, lanes]
            parts = (
                gram(left_w, right_w),
                gram(left_wx, right_w),
                gram(left_wxx, right_w),
                gram(left_w, right_wy),
                gram(left_wx, right_wy),
                gram(left_w, right_wyy),
            )
            for i, part in enumerate(parts):
                stats[p, :, i * n : (i + 1) * n, :] += part.reshape(shares, n, cols)

        for t in (4, 3, 5, 2, 6, 1, 7) if shares == 8 else range(1, shares):
            to = lax.rem(me_r + t, shares)
            copy = pltpu.make_async_remote_copy(
                src_ref=stats.at[p, to],
                dst_ref=held.at[p, t - 1],
                send_sem=part_send.at[p, t - 1],
                recv_sem=part_recv.at[p, t - 1],
                device_id={"refl": to},
                device_id_type=MESH,
            )
            copy.start()
            copies[p].append((t, copy))
    kept = pltpu.make_async_copy(msgs.at[0, me_s], returned.at[me_c, me_s], kept_sem)
    for p in range(2):
        total = stats[p, me_r]
        for t, copy in sorted(copies[p], key=lambda c: min(c[0], shares - c[0])):
            copy.wait_recv()
            total = total + held[p, t - 1]
        corr = pearson(*[total[i * n : (i + 1) * n] for i in range(6)])
        corr_ref[cores[p]] = corr
        flipped = corr.T
        lined = jnp.concatenate(
            [flipped[u * half : (u + 1) * half] for u in range(SUB)]
            + [jnp.zeros((half, 128 - SUB * n), jnp.float32)],
            1,
        )
        for s in range(half):
            msgs[p, s] = lined[s : s + 1]
        if p == 0:
            kept.start()

        @pl.loop(1 - p, half)
        def _(t):
            to = lax.rem(me_s + t, half)
            pltpu.make_async_remote_copy(
                src_ref=msgs.at[p, to],
                dst_ref=returned.at[me_c, me_s],
                send_sem=out_sem.at[p],
                recv_sem=in_sem.at[p],
                device_id={"dp": to * 2 + cores[p]},
                device_id_type=MESH,
            ).start()

    kept.wait()
    for p in range(2):
        for _, copy in copies[p]:
            copy.wait_send()
        many = pl.ds(0, half - 1 + p)
        pltpu.make_async_copy(landed.at[p, many], landed.at[p, many], send_sem.at[p]).wait()
        pltpu.make_async_copy(msgs.at[p, many], msgs.at[p, many], out_sem.at[p]).wait()
        pltpu.make_async_copy(returned.at[p, many], returned.at[p, many], in_sem.at[p]).wait()
    back_ref[...] = returned[...]


def whole(send, both, ops, shares):
    groups, eight, width = send.shape
    half = groups // 2
    blk = both.shape[0] // 2
    n = NOPS * (blk // shares)
    cols = half * SUB
    vmem = pl.BlockSpec(memory_space=pltpu.VMEM)
    dma = pltpu.SemaphoreType.DMA
    return pl.pallas_call(
        functools.partial(whole_kernel, shares, groups),
        out_shape=(
            jax.ShapeDtypeStruct((2, n, cols), jnp.float32),
            jax.ShapeDtypeStruct((2, half, 1, 128), jnp.float32),
        ),
        in_specs=[pl.BlockSpec(memory_space=pl.ANY), vmem, vmem],
        out_specs=[vmem, vmem],
        scratch_shapes=[
            pltpu.VMEM((2, half, eight, width), jnp.bfloat16),
            pltpu.VMEM((2, NOPS * blk, width), jnp.bfloat16),
            pltpu.VMEM((3, NOPS * blk, width), jnp.bfloat16),
            pltpu.VMEM((2, shares, 6 * n, cols), jnp.float32),
            pltpu.VMEM((2, shares - 1, 6 * n, cols), jnp.float32),
            pltpu.VMEM((2, half, 1, 128), jnp.float32),
            pltpu.VMEM((2, half, 1, 128), jnp.float32),
            dma((2,)),
            dma((2,)),
            dma,
            dma((2, shares - 1)),
            dma((2, shares - 1)),
            dma((2,)),
            dma((2,)),
            dma,
        ],
        compiler_params=pltpu.CompilerParams(
            collective_id=0, has_side_effects=True, vmem_limit_bytes=48 * 1024 * 1024
        ),
    )(send, both, ops)


def shards(intensities, observed, qweights, ops, pick):
    blk, width = intensities.shape
    groups = lax.axis_size("dp")
    shares = lax.axis_size("refl")
    rows = blk // shares
    own_w = (observed.astype(jnp.float32) * qweights.astype(jnp.float32)).astype(jnp.bfloat16)
    both = jnp.concatenate([intensities, own_w], 0)
    request = pick[:, 0][:, None] * SUB + jnp.arange(SUB, dtype=jnp.int32)[None, :]
    request = jnp.concatenate([request, request + blk], 1).reshape(-1)
    chosen = (request[:, None] == jnp.arange(2 * blk, dtype=jnp.int32)[None, :]).astype(jnp.bfloat16)
    send = jnp.dot(chosen, both, preferred_element_type=jnp.float32).astype(jnp.bfloat16)
    send = send.reshape(groups, 2 * SUB, width)
    corr, back = whole(send, both, ops, shares)
    corr = corr.reshape(2, NOPS, rows, SUB, groups // 2).transpose(1, 2, 4, 0, 3)
    corr = corr.reshape(NOPS, rows, groups * SUB)
    back = back[:, :, 0, : SUB * NOPS * rows].reshape(2, groups // 2, SUB, NOPS, rows)
    returned = back.transpose(3, 1, 0, 2, 4).reshape(NOPS, 1, groups, SUB, rows)
    return (corr, returned)


def solution(mesh):
    return jax.shard_map(
        shards,
        mesh=mesh,
        in_specs=(
            P("dp", "refl"),
            P("dp", "refl"),
            P("dp", "refl"),
            P(None, "refl"),
            P(None, "dp"),
        ),
        out_specs=(P(None, ("dp", "refl"), None), P(None, "dp", None, None, "refl")),
        check_vma=False,
    )
```

```python
import functools

import jax
import jax.numpy as jnp
from jax import lax
from jax.experimental import pallas as pl
from jax.experimental.pallas import tpu as pltpu
from jax.sharding import PartitionSpec as P

SUB = 4
NOPS = 4
MESH = pl.DeviceIdType.MESH


def gram(left, right):
    return lax.dot_general(
        left, right, (((1,), (1,)), ((), ())), preferred_element_type=jnp.float32
    )


def pearson(total_w, sum_x, sum_xx, sum_y, sum_xy, sum_yy):
    numer = total_w * sum_xy - sum_x * sum_y
    var_x = jnp.maximum(total_w * sum_xx - sum_x * sum_x, 0.05 * total_w * sum_xx)
    var_y = jnp.maximum(total_w * sum_yy - sum_y * sum_y, 0.05 * total_w * sum_yy)
    return numer / jnp.sqrt(var_x * var_y)


def whole_kernel(
    shares, groups, deep, block_ref, ops_ref, corr_ref, back_ref,
    ring, outbox, landed, moved, left, stats, held, msgs, returned,
    ring_send, ring_recv, send_sem, recv_sem, own_sem, part_send, part_recv, out_sem, in_sem, kept_sem,
):
    me_r = lax.axis_index("refl")
    me_d = lax.axis_index("dp")
    half = groups // 2
    tall = groups // deep
    quad = deep // 2
    me_c = lax.rem(me_d, 2)
    me_z = lax.rem(me_d // 2, deep)
    me_p = (me_d // (2 * deep)) * 2 + me_c
    width = block_ref.shape[2]
    blk = (block_ref.shape[0] - 1) * block_ref.shape[1] // 2
    rows = blk // shares
    n = NOPS * rows

    def device(p, z):
        return ((p // 2) * deep + z) * 2 + lax.rem(p, 2)

    barrier = pltpu.get_barrier_semaphore()
    for t in range(1, shares):
        pl.semaphore_signal(
            barrier, inc=1, device_id={"refl": lax.rem(me_r + t, shares)}, device_id_type=MESH
        )

    @pl.loop(1, groups)
    def _(t):
        pl.semaphore_signal(
            barrier, inc=1, device_id={"dp": lax.rem(me_d + t, groups)}, device_id_type=MESH
        )

    pl.semaphore_wait(barrier, shares - 1 + groups - 1)
    up = device(me_p, lax.rem(me_z + 1, deep))
    down = device(me_p, lax.rem(me_z + deep - 1, deep))
    far = quad - 1
    last = 2 * far
    cut = blk // 8
    tiles = 2 * cut + 1

    def hop(i, src, dst, to):
        copy = pltpu.make_async_remote_copy(
            src_ref=src,
            dst_ref=dst,
            send_sem=ring_send.at[i],
            recv_sem=ring_recv.at[i],
            device_id={"dp": to},
            device_id_type=MESH,
        )
        copy.start()
        return copy

    def hop_up(j):
        src = block_ref if j == 1 else ring.at[j - 2]
        if j <= far:
            return hop(j - 1, src, ring.at[j - 1], up)
        part = pl.ds(0, cut)
        return hop(j - 1, src.at[part], ring.at[last, part], up)

    def hop_down(j):
        src = block_ref if j == 1 else ring.at[far + j - 2]
        if j <= far:
            return hop(quad + j - 1, src, ring.at[far + j - 1], down)
        part = pl.ds(cut, tiles - cut)
        return hop(quad + j - 1, src.at[part], ring.at[last, part], down)

    row_at = lax.broadcasted_iota(jnp.int32, (tall * 8, 128), 0)
    lane_at = lax.broadcasted_iota(jnp.int32, (tall * 8, 128), 1)
    asks = lane_at == device(row_at // 8, me_z)
    row_in = (lax.rem(row_at // SUB, 2) * blk + lax.rem(row_at, SUB)).astype(jnp.float32)[:, : 2 * blk]
    lane_in = lane_at.astype(jnp.float32)[:, : 2 * blk]
    waiting = {}

    def rows_of(ref):
        return ref[: 2 * cut].astype(jnp.float32).reshape(2 * blk, width).astype(jnp.bfloat16)

    def serve(offset, ref):
        w = (offset + quad - 2) % deep
        p, q = w // quad, w % quad
        line = ref[2 * cut, :, :128].astype(jnp.float32)[0:1]
        asked = jnp.sum(jnp.where(asks, line, 0.0), axis=1, keepdims=True)
        chosen = (lane_in == row_in + asked * SUB).astype(jnp.float32).astype(jnp.bfloat16)
        got = jnp.dot(chosen, rows_of(ref), preferred_element_type=jnp.float32)
        outbox[w] = got.reshape(tall, 8, width).astype(jnp.bfloat16)
        own = pltpu.make_async_copy(
            outbox.at[w, me_p], landed.at[p, me_p * quad + q], own_sem.at[w]
        )
        own.start()
        waiting[w] = own

        @pl.loop(1, tall)
        def _(t):
            to = lax.rem(me_p + t, tall)
            pltpu.make_async_remote_copy(
                src_ref=outbox.at[w, to],
                dst_ref=landed.at[p, me_p * quad + q],
                send_sem=send_sem.at[p],
                recv_sem=recv_sem.at[p],
                device_id={"dp": device(to, me_z)},
                device_id_type=MESH,
            ).start()

    step = 256

    def operate(k):
        line = ops_ref[k : k + 1, :] - me_r * width
        both = rows_of(block_ref)

        @pl.loop(0, width // step)
        def _(g):
            at = lax.broadcasted_iota(jnp.int32, (step, width), 0) + g * step
            place = (at == line).astype(jnp.float32).astype(jnp.bfloat16)
            lanes = pl.ds(pl.multiple_of(g * step, step), step)
            put = gram(both, place).astype(jnp.bfloat16)
            moved[0, k * blk : (k + 1) * blk, lanes] = put[:blk]
            moved[1, k * blk : (k + 1) * blk, lanes] = put[blk:]

    tile = 512

    def weigh():
        to_row = lax.broadcasted_iota(jnp.int32, (NOPS * blk, NOPS * blk), 0)
        from_row = lax.broadcasted_iota(jnp.int32, (NOPS * blk, NOPS * blk), 1)
        want = ((to_row // rows) % NOPS) * blk + (to_row // n) * rows + to_row % rows
        order = (from_row == want).astype(jnp.float32).astype(jnp.bfloat16)

        @pl.loop(0, width // tile)
        def _(g):
            lanes = pl.ds(pl.multiple_of(g * tile, tile), tile)
            own_x = jnp.dot(order, moved[0, :, lanes], preferred_element_type=jnp.float32)
            own_w = jnp.dot(order, moved[1, :, lanes], preferred_element_type=jnp.float32)
            own_wx = own_w * own_x
            left[0, :, lanes] = own_w.astype(jnp.bfloat16)
            left[1, :, lanes] = own_wx.astype(jnp.bfloat16)
            left[2, :, lanes] = (own_wx * own_x).astype(jnp.bfloat16)

    cols = half * SUB
    height = half * 2 * SUB
    at = lax.broadcasted_iota(jnp.int32, (cols, height), 0)
    source = lax.broadcasted_iota(jnp.int32, (cols, height), 1)
    wanted = (at % half) * (2 * SUB) + at // half
    pick_x = (source == wanted).astype(jnp.float32).astype(jnp.bfloat16)
    pick_w = (source == wanted + SUB).astype(jnp.float32).astype(jnp.bfloat16)
    copies = [[], []]

    def sums(p):
        for w in range(p * quad, (p + 1) * quad):
            waiting[w].wait()
        many = pl.ds(0, quad * (tall - 1))
        pltpu.make_async_copy(landed.at[p, many], landed.at[p, many], recv_sem.at[p]).wait()
        stats[p] = jnp.zeros(stats.shape[1:], jnp.float32)

        @pl.loop(0, width // tile)
        def _(g):
            lanes = pl.ds(pl.multiple_of(g * tile, tile), tile)
            got = landed[p, :, :, lanes].astype(jnp.float32).reshape(height, tile).astype(jnp.bfloat16)
            got_x = jnp.dot(pick_x, got, preferred_element_type=jnp.float32)
            got_w = jnp.dot(pick_w, got, preferred_element_type=jnp.float32)
            right_w = got_w.astype(jnp.bfloat16)
            wy = got_w * got_x
            right_wy = wy.astype(jnp.bfloat16)
            right_wyy = (wy * got_x).astype(jnp.bfloat16)
            left_w = left[0, :, lanes]
            left_wx = left[1, :, lanes]
            left_wxx = left[2, :, lanes]
            parts = (
                gram(left_w, right_w),
                gram(left_wx, right_w),
                gram(left_wxx, right_w),
                gram(left_w, right_wy),
                gram(left_wx, right_wy),
                gram(left_w, right_wyy),
            )
            for i, part in enumerate(parts):
                stats[p, :, i * n : (i + 1) * n, :] += part.reshape(shares, n, cols)

        for t in (4, 3, 5, 2, 6, 1, 7) if shares == 8 else range(1, shares):
            to = lax.rem(me_r + t, shares)
            copy = pltpu.make_async_remote_copy(
                src_ref=stats.at[p, to],
                dst_ref=held.at[p, t - 1],
                send_sem=part_send.at[p, t - 1],
                recv_sem=part_recv.at[p, t - 1],
                device_id={"refl": to},
                device_id_type=MESH,
            )
            copy.start()
            copies[p].append((t, copy))
    hops = [hop_up(1), hop_down(1)]
    serve(0, block_ref)
    operate(0)
    operate(1)
    for j in range(1, quad):
        above, below = hops[-2:]
        above.wait_recv()
        hops.append(hop_up(j + 1))
        below.wait_recv()
        hops.append(hop_down(j + 1))
        serve(-j, ring.at[j - 1])
        serve(j, ring.at[far + j - 1])
        if j == 1:
            operate(2)
        elif j == 2:
            operate(3)
            weigh()
    sums(0)
    for copy in hops[-2:]:
        copy.wait_recv()
    serve(quad, ring.at[last])
    sums(1)
    kept = pltpu.make_async_copy(msgs.at[me_d], returned.at[me_d], kept_sem)
    for p in range(2):
        total = stats[p, me_r]
        for t, copy in sorted(copies[p], key=lambda c: min(c[0], shares - c[0])):
            copy.wait_recv()
            total = total + held[p, t - 1]
        corr = pearson(*[total[i * n : (i + 1) * n] for i in range(6)])
        flipped = corr.T
        lined = jnp.concatenate(
            [flipped[u * half : (u + 1) * half] for u in range(SUB)]
            + [jnp.zeros((half, 128 - SUB * n), jnp.float32)],
            1,
        )
        for i in range(half):
            z = lax.rem(me_z + p * quad + i % quad - (quad - 2) + deep, deep)
            msgs[device(i // quad, z)] = lined[i : i + 1]
        if p == 0:
            kept.start()

        @pl.loop(0, quad)
        def _(q):
            z = lax.rem(me_z + p * quad + q - (quad - 2) + deep, deep)

            @pl.loop(0, tall)
            def _(t):
                to = device(lax.rem(me_p + t, tall), z)

                @pl.when(to != me_d)
                def _():
                    pltpu.make_async_remote_copy(
                        src_ref=msgs.at[to],
                        dst_ref=returned.at[me_d],
                        send_sem=out_sem.at[p],
                        recv_sem=in_sem.at[p],
                        device_id={"dp": to},
                        device_id_type=MESH,
                    ).start()

    corr_ref[...] = msgs[...]
    kept.wait()
    for copy in hops:
        copy.wait_send()
    for p in range(2):
        for _, copy in copies[p]:
            copy.wait_send()
        many = pl.ds(0, quad * (tall - 1))
        pltpu.make_async_copy(landed.at[p, many], landed.at[p, many], send_sem.at[p]).wait()
        many = pl.ds(0, half - 1 + p)
        pltpu.make_async_copy(msgs.at[many], msgs.at[many], out_sem.at[p]).wait()
    for p in range(2):
        many = pl.ds(0, half - 1 + p)
        pltpu.make_async_copy(returned.at[many], returned.at[many], in_sem.at[p]).wait()
    back_ref[...] = returned[...]


def whole(block, ops, shares, groups):
    tiles, eight, width = block.shape
    deep = 8
    half = groups // 2
    blk = (tiles - 1) * eight // 2
    n = NOPS * (blk // shares)
    cols = half * SUB
    vmem = pl.BlockSpec(memory_space=pltpu.VMEM)
    dma = pltpu.SemaphoreType.DMA
    return pl.pallas_call(
        functools.partial(whole_kernel, shares, groups, deep),
        out_shape=(jax.ShapeDtypeStruct((groups, 1, 128), jnp.float32),) * 2,
        in_specs=[vmem, vmem],
        out_specs=[vmem, vmem],
        scratch_shapes=[
            pltpu.VMEM((deep - 1, tiles, eight, width), jnp.bfloat16),
            pltpu.VMEM((deep, groups // deep, eight, width), jnp.bfloat16),
            pltpu.VMEM((2, half, eight, width), jnp.bfloat16),
            pltpu.VMEM((2, NOPS * blk, width), jnp.bfloat16),
            pltpu.VMEM((3, NOPS * blk, width), jnp.bfloat16),
            pltpu.VMEM((2, shares, 6 * n, cols), jnp.float32),
            pltpu.VMEM((2, shares - 1, 6 * n, cols), jnp.float32),
            pltpu.VMEM((groups, 1, 128), jnp.float32),
            pltpu.VMEM((groups, 1, 128), jnp.float32),
            dma((deep,)),
            dma((deep,)),
            dma((2,)),
            dma((2,)),
            dma((deep,)),
            dma((2, shares - 1)),
            dma((2, shares - 1)),
            dma((2,)),
            dma((2,)),
            dma,
        ],
        compiler_params=pltpu.CompilerParams(
            collective_id=0, has_side_effects=True, vmem_limit_bytes=48 * 1024 * 1024
        ),
    )(block, ops)


def shards(intensities, observed, qweights, ops, pick):
    blk, width = intensities.shape
    groups = lax.axis_size("dp")
    shares = lax.axis_size("refl")
    rows = blk // shares
    own_w = (observed.astype(jnp.float32) * qweights.astype(jnp.float32)).astype(jnp.bfloat16)
    asks = jnp.pad(pick.T.astype(jnp.bfloat16), ((0, 7), (0, width - groups)))
    block = jnp.concatenate([intensities, own_w, asks], 0).reshape(-1, 8, width)
    corr, back = whole(block, ops, shares, groups)
    used = SUB * NOPS * rows
    corr = corr[:, 0, :used].reshape(groups, SUB, NOPS, rows).transpose(2, 3, 0, 1)
    corr = corr.reshape(NOPS, rows, groups * SUB)
    back = back[:, 0, :used].reshape(groups, SUB, NOPS, rows)
    returned = back.transpose(2, 0, 1, 3)[:, None]
    return (corr, returned)


def solution(mesh):
    return jax.shard_map(
        shards,
        mesh=mesh,
        in_specs=(
            P("dp", "refl"),
            P("dp", "refl"),
            P("dp", "refl"),
            P(None, "refl"),
            P(None, "dp"),
        ),
        out_specs=(P(None, ("dp", "refl"), None), P(None, "dp", None, None, "refl")),
        check_vma=False,
    )
```

```python
import functools

import jax
import jax.numpy as jnp
from jax import lax
from jax.experimental import pallas as pl
from jax.experimental.pallas import tpu as pltpu
from jax.sharding import PartitionSpec as P

SUB = 4
NOPS = 4
MESH = pl.DeviceIdType.MESH


def gram(left, right):
    return lax.dot_general(
        left, right, (((1,), (1,)), ((), ())), preferred_element_type=jnp.float32
    )


def pearson(total_w, sum_x, sum_xx, sum_y, sum_xy, sum_yy):
    numer = total_w * sum_xy - sum_x * sum_y
    var_x = jnp.maximum(total_w * sum_xx - sum_x * sum_x, 0.05 * total_w * sum_xx)
    var_y = jnp.maximum(total_w * sum_yy - sum_y * sum_y, 0.05 * total_w * sum_yy)
    return numer / jnp.sqrt(var_x * var_y)


def whole_kernel(
    shares, groups, deep, block_ref, ops_ref, corr_ref, back_ref,
    ring, outbox, landed, moved, left, stats, held, msgs, returned,
    ring_send, ring_recv, send_sem, recv_sem, own_sem, part_send, part_recv, out_sem, in_sem, kept_sem,
):
    me_r = lax.axis_index("refl")
    me_d = lax.axis_index("dp")
    half = groups // 2
    tall = groups // deep
    quad = deep // 2
    me_c = lax.rem(me_d, 2)
    me_z = lax.rem(me_d // 2, deep)
    me_p = (me_d // (2 * deep)) * 2 + me_c
    width = block_ref.shape[2]
    blk = (block_ref.shape[0] - 1) * block_ref.shape[1] // 2
    rows = blk // shares
    n = NOPS * rows

    def device(p, z):
        return ((p // 2) * deep + z) * 2 + lax.rem(p, 2)

    barrier = pltpu.get_barrier_semaphore()
    for t in range(1, shares):
        pl.semaphore_signal(
            barrier, inc=1, device_id={"refl": lax.rem(me_r + t, shares)}, device_id_type=MESH
        )

    @pl.loop(1, tall)
    def _(t):
        to = device(lax.rem(me_p + t, tall), me_z)
        pl.semaphore_signal(barrier, inc=1, device_id={"dp": to}, device_id_type=MESH)

    for t in (1, deep - 1):
        to = device(me_p, lax.rem(me_z + t, deep))
        pl.semaphore_signal(barrier, inc=1, device_id={"dp": to}, device_id_type=MESH)
    pl.semaphore_wait(barrier, shares - 1 + tall - 1 + 2)
    up = device(me_p, lax.rem(me_z + 1, deep))
    down = device(me_p, lax.rem(me_z + deep - 1, deep))
    far = quad - 1
    last = 2 * far
    cut = blk // 8
    tiles = 2 * cut + 1

    def hop(i, src, dst, to):
        copy = pltpu.make_async_remote_copy(
            src_ref=src,
            dst_ref=dst,
            send_sem=ring_send.at[i],
            recv_sem=ring_recv.at[i],
            device_id={"dp": to},
            device_id_type=MESH,
        )
        copy.start()
        return copy

    parts_of = (pl.ds(0, cut), pl.ds(cut, tiles - cut))

    def hop_up(j, h):
        src = block_ref if j == 1 else ring.at[j - 2]
        dst = ring.at[j - 1 if j <= far else last]
        return hop(2 * (j - 1) + h, src.at[parts_of[h]], dst.at[parts_of[h]], up)

    def hop_down(j, h):
        src = block_ref if j == 1 else ring.at[far + j - 2]
        dst = ring.at[far + j - 1 if j <= far else last]
        return hop(2 * (quad + j - 1) + h, src.at[parts_of[h]], dst.at[parts_of[h]], down)

    row_at = lax.broadcasted_iota(jnp.int32, (tall * 8, 128), 0)
    lane_at = lax.broadcasted_iota(jnp.int32, (tall * 8, 128), 1)
    asks = lane_at == device(row_at // 8, me_z)
    row_in = (lax.rem(row_at // SUB, 2) * blk + lax.rem(row_at, SUB)).astype(jnp.float32)[:, : 2 * blk]
    lane_in = lane_at.astype(jnp.float32)[:, : 2 * blk]
    waiting = {}

    def rows_of(ref):
        return ref[: 2 * cut].astype(jnp.float32).reshape(2 * blk, width).astype(jnp.bfloat16)

    def serve(offset, ref):
        w = (offset + quad - 2) % deep
        p, q = w // quad, w % quad
        line = ref[2 * cut, :, :128].astype(jnp.float32)[0:1]
        asked = jnp.sum(jnp.where(asks, line, 0.0), axis=1, keepdims=True)
        chosen = (lane_in == row_in + asked * SUB).astype(jnp.float32).astype(jnp.bfloat16)
        got = jnp.dot(chosen, rows_of(ref), preferred_element_type=jnp.float32)
        outbox[w] = got.reshape(tall, 8, width).astype(jnp.bfloat16)
        own = pltpu.make_async_copy(
            outbox.at[w, me_p], landed.at[p, me_p * quad + q], own_sem.at[w]
        )
        own.start()
        waiting[w] = own

        @pl.loop(1, tall)
        def _(t):
            to = lax.rem(me_p + t, tall)
            pltpu.make_async_remote_copy(
                src_ref=outbox.at[w, to],
                dst_ref=landed.at[p, me_p * quad + q],
                send_sem=send_sem.at[p],
                recv_sem=recv_sem.at[p],
                device_id={"dp": device(to, me_z)},
                device_id_type=MESH,
            ).start()

    step = 256

    def operate(k):
        line = ops_ref[k : k + 1, :] - me_r * width
        both = rows_of(block_ref)

        @pl.loop(0, width // step)
        def _(g):
            at = lax.broadcasted_iota(jnp.int32, (step, width), 0) + g * step
            place = (at == line).astype(jnp.float32).astype(jnp.bfloat16)
            lanes = pl.ds(pl.multiple_of(g * step, step), step)
            put = gram(both, place).astype(jnp.bfloat16)
            moved[0, k * blk : (k + 1) * blk, lanes] = put[:blk]
            moved[1, k * blk : (k + 1) * blk, lanes] = put[blk:]

    tile = 512

    def weigh():
        to_row = lax.broadcasted_iota(jnp.int32, (NOPS * blk, NOPS * blk), 0)
        from_row = lax.broadcasted_iota(jnp.int32, (NOPS * blk, NOPS * blk), 1)
        want = ((to_row // rows) % NOPS) * blk + (to_row // n) * rows + to_row % rows
        order = (from_row == want).astype(jnp.float32).astype(jnp.bfloat16)

        @pl.loop(0, width // tile)
        def _(g):
            lanes = pl.ds(pl.multiple_of(g * tile, tile), tile)
            own_x = jnp.dot(order, moved[0, :, lanes], preferred_element_type=jnp.float32)
            own_w = jnp.dot(order, moved[1, :, lanes], preferred_element_type=jnp.float32)
            own_wx = own_w * own_x
            left[0, :, lanes] = own_w.astype(jnp.bfloat16)
            left[1, :, lanes] = own_wx.astype(jnp.bfloat16)
            left[2, :, lanes] = (own_wx * own_x).astype(jnp.bfloat16)

    cols = half * SUB
    height = half * 2 * SUB
    at = lax.broadcasted_iota(jnp.int32, (cols, height), 0)
    source = lax.broadcasted_iota(jnp.int32, (cols, height), 1)
    wanted = (at % half) * (2 * SUB) + at // half
    pick_x = (source == wanted).astype(jnp.float32).astype(jnp.bfloat16)
    pick_w = (source == wanted + SUB).astype(jnp.float32).astype(jnp.bfloat16)
    copies = [[], []]

    def sums(p):
        for w in range(p * quad, (p + 1) * quad):
            waiting[w].wait()
        many = pl.ds(0, quad * (tall - 1))
        pltpu.make_async_copy(landed.at[p, many], landed.at[p, many], recv_sem.at[p]).wait()
        stats[p] = jnp.zeros(stats.shape[1:], jnp.float32)

        @pl.loop(0, width // tile)
        def _(g):
            lanes = pl.ds(pl.multiple_of(g * tile, tile), tile)
            got = landed[p, :, :, lanes].astype(jnp.float32).reshape(height, tile).astype(jnp.bfloat16)
            got_x = jnp.dot(pick_x, got, preferred_element_type=jnp.float32)
            got_w = jnp.dot(pick_w, got, preferred_element_type=jnp.float32)
            right_w = got_w.astype(jnp.bfloat16)
            wy = got_w * got_x
            right_wy = wy.astype(jnp.bfloat16)
            right_wyy = (wy * got_x).astype(jnp.bfloat16)
            left_w = left[0, :, lanes]
            left_wx = left[1, :, lanes]
            left_wxx = left[2, :, lanes]
            parts = (
                gram(left_w, right_w),
                gram(left_wx, right_w),
                gram(left_wxx, right_w),
                gram(left_w, right_wy),
                gram(left_wx, right_wy),
                gram(left_w, right_wyy),
            )
            for i, part in enumerate(parts):
                stats[p, :, i * n : (i + 1) * n, :] += part.reshape(shares, n, cols)

        for t in (4, 3, 5, 2, 6, 1, 7) if shares == 8 else range(1, shares):
            to = lax.rem(me_r + t, shares)
            copy = pltpu.make_async_remote_copy(
                src_ref=stats.at[p, to],
                dst_ref=held.at[p, t - 1],
                send_sem=part_send.at[p, t - 1],
                recv_sem=part_recv.at[p, t - 1],
                device_id={"refl": to},
                device_id_type=MESH,
            )
            copy.start()
            copies[p].append((t, copy))
    hops = []
    flying = {}

    def fly(go, j, h):
        copy = go(j, h)
        hops.append(copy)
        flying[go, j, h] = copy

    for h in range(2):
        fly(hop_up, 1, h)
        fly(hop_down, 1, 1 - h)
    serve(0, block_ref)
    operate(0)
    operate(1)
    for j in range(1, quad):
        for h in range(2):
            for go, part in ((hop_up, h), (hop_down, 1 - h)):
                flying[go, j, part].wait_recv()
                if j < far or h == 0:
                    fly(go, j + 1, part)
        serve(-j, ring.at[j - 1])
        serve(j, ring.at[far + j - 1])
        if j == 1:
            operate(2)
        elif j == 2:
            operate(3)
            weigh()
    sums(0)
    flying[hop_up, quad, 0].wait_recv()
    flying[hop_down, quad, 1].wait_recv()
    serve(quad, ring.at[last])
    sums(1)
    kept = pltpu.make_async_copy(msgs.at[me_d], returned.at[me_d], kept_sem)
    for p in range(2):
        total = stats[p, me_r]
        for t, copy in sorted(copies[p], key=lambda c: min(c[0], shares - c[0])):
            copy.wait_recv()
            total = total + held[p, t - 1]
        corr = pearson(*[total[i * n : (i + 1) * n] for i in range(6)])
        flipped = corr.T
        lined = jnp.concatenate(
            [flipped[u * half : (u + 1) * half] for u in range(SUB)]
            + [jnp.zeros((half, 128 - SUB * n), jnp.float32)],
            1,
        )
        for i in range(half):
            z = lax.rem(me_z + p * quad + i % quad - (quad - 2) + deep, deep)
            msgs[device(i // quad, z)] = lined[i : i + 1]
        if p == 0:
            kept.start()

        @pl.loop(0, quad)
        def _(q):
            z = lax.rem(me_z + p * quad + q - (quad - 2) + deep, deep)

            @pl.loop(0, tall)
            def _(t):
                to = device(lax.rem(me_p + t, tall), z)

                @pl.when(to != me_d)
                def _():
                    pltpu.make_async_remote_copy(
                        src_ref=msgs.at[to],
                        dst_ref=returned.at[me_d],
                        send_sem=out_sem.at[p],
                        recv_sem=in_sem.at[p],
                        device_id={"dp": to},
                        device_id_type=MESH,
                    ).start()

    corr_ref[...] = msgs[...]
    kept.wait()
    for copy in hops:
        copy.wait_send()
    for p in range(2):
        for _, copy in copies[p]:
            copy.wait_send()
        many = pl.ds(0, quad * (tall - 1))
        pltpu.make_async_copy(landed.at[p, many], landed.at[p, many], send_sem.at[p]).wait()
        many = pl.ds(0, half - 1 + p)
        pltpu.make_async_copy(msgs.at[many], msgs.at[many], out_sem.at[p]).wait()
    for p in range(2):
        many = pl.ds(0, half - 1 + p)
        pltpu.make_async_copy(returned.at[many], returned.at[many], in_sem.at[p]).wait()
    back_ref[...] = returned[...]


def whole(block, ops, shares, groups):
    tiles, eight, width = block.shape
    deep = 8
    half = groups // 2
    blk = (tiles - 1) * eight // 2
    n = NOPS * (blk // shares)
    cols = half * SUB
    vmem = pl.BlockSpec(memory_space=pltpu.VMEM)
    dma = pltpu.SemaphoreType.DMA
    return pl.pallas_call(
        functools.partial(whole_kernel, shares, groups, deep),
        out_shape=(jax.ShapeDtypeStruct((groups, 1, 128), jnp.float32),) * 2,
        in_specs=[vmem, vmem],
        out_specs=[vmem, vmem],
        scratch_shapes=[
            pltpu.VMEM((deep - 1, tiles, eight, width), jnp.bfloat16),
            pltpu.VMEM((deep, groups // deep, eight, width), jnp.bfloat16),
            pltpu.VMEM((2, half, eight, width), jnp.bfloat16),
            pltpu.VMEM((2, NOPS * blk, width), jnp.bfloat16),
            pltpu.VMEM((3, NOPS * blk, width), jnp.bfloat16),
            pltpu.VMEM((2, shares, 6 * n, cols), jnp.float32),
            pltpu.VMEM((2, shares - 1, 6 * n, cols), jnp.float32),
            pltpu.VMEM((groups, 1, 128), jnp.float32),
            pltpu.VMEM((groups, 1, 128), jnp.float32),
            dma((2 * deep,)),
            dma((2 * deep,)),
            dma((2,)),
            dma((2,)),
            dma((deep,)),
            dma((2, shares - 1)),
            dma((2, shares - 1)),
            dma((2,)),
            dma((2,)),
            dma,
        ],
        compiler_params=pltpu.CompilerParams(
            collective_id=0, has_side_effects=True, vmem_limit_bytes=48 * 1024 * 1024
        ),
    )(block, ops)


def shards(intensities, observed, qweights, ops, pick):
    blk, width = intensities.shape
    groups = lax.axis_size("dp")
    shares = lax.axis_size("refl")
    rows = blk // shares
    own_w = (observed.astype(jnp.float32) * qweights.astype(jnp.float32)).astype(jnp.bfloat16)
    asks = jnp.pad(pick.T.astype(jnp.bfloat16), ((0, 7), (0, width - groups)))
    block = jnp.concatenate([intensities, own_w, asks], 0).reshape(-1, 8, width)
    corr, back = whole(block, ops, shares, groups)
    used = SUB * NOPS * rows
    corr = corr[:, 0, :used].reshape(groups, SUB, NOPS, rows).transpose(2, 3, 0, 1)
    corr = corr.reshape(NOPS, rows, groups * SUB)
    back = back[:, 0, :used].reshape(groups, SUB, NOPS, rows)
    returned = back.transpose(2, 0, 1, 3)[:, None]
    return (corr, returned)


def solution(mesh):
    return jax.shard_map(
        shards,
        mesh=mesh,
        in_specs=(
            P("dp", "refl"),
            P("dp", "refl"),
            P("dp", "refl"),
            P(None, "refl"),
            P(None, "dp"),
        ),
        out_specs=(P(None, ("dp", "refl"), None), P(None, "dp", None, None, "refl")),
        check_vma=False,
    )
```
